32 devices in a mesh: section: 4 (over z), dp: 4 (over x, core), mp: 2 (over y).
Axes of the slice: x: 2, y: 2, z: 4, core: 2. Of those that a mesh axis runs over, the one named last changes fastest.
Arguments:
- hidden: bfloat16 [4, 16, 4, 4096], P('section', 'mp', 'dp'), may hold values from -2048 to 2048
- token_ids: int32 [16, 4], P('mp', 'dp'), may hold values from 0 to 8191
- seq_lengths: int32 [4], replicated, may hold values from 1 to 16, 21 in all
- head_slices: bfloat16 [4, 4096, 8192], P('section', None, ('dp', 'mp')), may hold values from -8 to 8
- value_head: bfloat16 [4, 4096], P('section'), may hold values from -0.09375 to 0.09375
Outputs:
- scores: float32 [4, 16, 4], P('section', 'mp', 'dp')
- advantages: float32 [16, 4], P('mp', 'dp')
- trunk_grad: bfloat16 [4, 16, 4, 4096], P('section', 'mp', 'dp')
The draws below stay inside these ranges and needn't reach their ends.
Inputs may be any that keep to these rules, and one draw needn't show every extreme that they name: Sequence j is live at positions 0 to seq_lengths[j] - 1; the lengths sum to 21 and one of them is 16.
All inputs are finite; a program needn't handle non-finite values.
Results may differ from the reference program's by a relative error of at most 0.0047.
Values may be sent and summed in bfloat16 or wider, within the bound.
A program may use at most 64 MiB of HBM per device.

```python
import math
import jax
import jax.numpy as jnp
import numpy as np
from jax import lax

D = 4096
LEN = 16
SEQS = 4
VOCAB = 8192
N_SECTION = 4


def head_scales(key):
    base_key = jax.random.fold_in(key, 911)
    sigma = 3.0 / math.sqrt(D)
    col_scale = jnp.ones((VOCAB,), jnp.float32)
    return (base_key, sigma, col_scale)


def head_noise(base_key, number):
    return jnp.clip(jax.random.normal(jax.random.fold_in(base_key, number), (D, VOCAB), jnp.float32), -6.0, 6.0)


def draw_head_slices(key, part):
    base_key, sigma, col_scale = head_scales(key)
    factor = (sigma * col_scale)[None, :]
    base_head = head_noise(base_key, 0)
    behaviour_noise = 0.25 * head_noise(base_key, 1)
    behaviour = ((base_head + behaviour_noise) * factor).astype(jnp.bfloat16)
    implicit = ((base_head + 0.3 * head_noise(base_key, 2)) * factor).astype(jnp.bfloat16)
    anchor = (base_head * factor).astype(jnp.bfloat16)
    current = ((base_head + behaviour_noise + 0.05 * head_noise(base_key, 3)) * factor).astype(jnp.bfloat16)
    return jnp.stack([behaviour, implicit, anchor, current])


def draw_hidden(key, part):
    dims_of = (N_SECTION, LEN, SEQS, D)
    hidden_rows = jnp.clip(jax.random.normal(jax.random.fold_in(key, 17), dims_of, jnp.float32), -6.0, 6.0)
    return hidden_rows.astype(jnp.bfloat16)


def with_ends(entries, own_key, least, largest):
    longest = entries.shape.index(max(entries.shape))
    spots = []
    for shift in (0, 1):
        where = [jax.random.randint(jax.random.fold_in(own_key, axis), (), 0, length) for axis, length in enumerate(entries.shape)]
        where[longest] = (where[longest] + shift) % entries.shape[longest]
        spots.append(tuple(where))
    return entries.at[spots[0]].set(least).at[spots[1]].set(largest)


def levels(own_key, extent, shards, smallest, largest):
    def one(axis_at, blocks):
        heights = jax.random.uniform(jax.random.fold_in(jax.random.fold_in(own_key, 6), axis_at), (blocks,), jnp.float32, smallest / len(shards), largest / len(shards))
        return jnp.repeat(jnp.exp(heights), extent[axis_at] // blocks).reshape((-1,) + (1,) * (len(extent) - axis_at - 1))

    gain = one(*shards[0])
    for cut in shards[1:]:
        gain = gain * one(*cut)
    return gain


def cumulative_ranks(number_of, skew):
    loads = [(1 << 20) // math.isqrt(grade ** skew) + 1 for grade in range(1, number_of + 1)]
    scale = 1 + sum(loads) // (1 << 30)
    return np.cumsum(np.array([max(1, weight // scale) for weight in loads]))


def ranked(stream_key, dims, count, skew):
    table = cumulative_ranks(count, skew)
    ticket = jax.random.randint(jax.random.fold_in(stream_key, 1), dims, 0, int(table[count - 1]))
    rank = jnp.searchsorted(jnp.asarray(table, jnp.int32), ticket, side="right")
    return jax.random.permutation(jax.random.fold_in(stream_key, 2), count)[rank].astype(jnp.int32)


def length_profile(number_of, total, limit, skew):
    portions = [(1 << 20) // math.isqrt(rank ** skew) + 1 for rank in range(2, number_of + 1)]
    rest, counts = total - limit - (number_of - 1), [1] * (number_of - 1)
    while rest > 0:
        movable = [i for i in range(number_of - 1) if counts[i] < limit]
        mass, budget = sum([portions[i] for i in movable]), rest
        for i in movable:
            more = min(limit - counts[i], max(1, budget * portions[i] // mass), rest)
            counts[i] = counts[i] + more
            rest = rest - more
    return np.array([limit] + counts)


def ragged_sizes(own_key, amount, total, bound, skew):
    if amount == 2:
        one = jax.random.randint(own_key, (), max(1, total - bound), min(bound, total - 1) + 1)
        return jnp.stack([one, total - one])
    sizes = jnp.asarray(length_profile(amount, total, bound, skew), jnp.int32)
    twos = (amount - 1) // 2
    source_of, receiver = sizes[1:1 + 2 * twos:2], sizes[2:2 + 2 * twos:2]
    slack = jnp.minimum(source_of - 1, bound - receiver)
    passed = jax.random.randint(jax.random.fold_in(own_key, 1), (twos,), 0, 1 << 20) % (slack + 1)
    sizes = sizes.at[1:1 + 2 * twos:2].set(source_of - passed).at[2:2 + 2 * twos:2].set(receiver + passed)
    return sizes[jax.random.permutation(jax.random.fold_in(own_key, 2), amount)]


def scatter_about(stream_key, extent, scale, limit, shards=(), kind=jnp.bfloat16):
    values = scale * jax.random.normal(stream_key, extent, jnp.float32)
    if shards:
        values = values * levels(stream_key, extent, shards, -0.22, 0.18)
    return jnp.clip(values, -limit, limit).astype(kind)


def setup_inputs(seed: int = 0) -> dict:
    splits = jax.random.split(jax.random.key(seed), 6)
    hidden = draw_hidden(jax.random.fold_in(splits[5], 71), 0)
    token_ids = with_ends(ranked(splits[1], (LEN, SEQS), VOCAB, 2), jax.random.fold_in(splits[1], 3), 0, VOCAB - 1).astype(jnp.int32)
    seq_lengths = ragged_sizes(splits[2], SEQS, SEQS * LEN // 3, LEN, 2).astype(jnp.int32)
    head_slices = draw_head_slices(jax.random.fold_in(splits[5], 71), 0)
    value_head = scatter_about(splits[4], (N_SECTION, D), D ** -0.5, 0.09375, ((0, 4),))
    return dict(hidden=hidden, token_ids=token_ids, seq_lengths=seq_lengths, head_slices=head_slices, value_head=value_head)


gae_decay = 0.95
reward_gain = 0.5
drift_gain = 0.1
penalty_gain = 0.2
loss_scale = 16.0


def token_scores(flat_rows, flat_ids, head_part):
    logits = jnp.dot(flat_rows, head_part, preferred_element_type=jnp.float32)
    maximum = jnp.max(logits, axis=1)
    log_norm = maximum + jnp.log(jnp.sum(jnp.exp(logits - maximum[:, None]), axis=1))
    picked = jnp.take_along_axis(logits, flat_ids[:, None], axis=1)[:, 0]
    return picked - log_norm, log_norm, logits


def reference(hidden, token_ids, seq_lengths, head_slices, value_head):
    flat_rows = hidden[0].reshape(LEN * SEQS, D)
    flat_ids = token_ids.reshape(LEN * SEQS).astype(jnp.int32)
    positions = lax.broadcasted_iota(jnp.int32, (LEN, SEQS), 0)
    live_mask = positions < seq_lengths[None, :].astype(jnp.int32)
    live_float = live_mask.astype(jnp.float32)
    score_list = []
    for section_index in range(N_SECTION):
        log_prob, log_norm, logits = token_scores(flat_rows, flat_ids, head_slices[section_index])
        score_list.append(jnp.where(live_mask, log_prob.reshape(LEN, SEQS), jnp.float32(0.0)))
    scores = jnp.stack(score_list)
    critic = jnp.dot(flat_rows, value_head[1], preferred_element_type=jnp.float32).reshape(LEN, SEQS)
    reward = reward_gain * (scores[1] - scores[2]) - drift_gain * (scores[0] - scores[2])
    next_values = jnp.concatenate([critic[1:], jnp.zeros((1, SEQS), jnp.float32)], axis=0)
    next_mask = jnp.concatenate([live_float[1:], jnp.zeros((1, SEQS), jnp.float32)], axis=0)
    td_error = live_float * (reward + next_mask * next_values - critic)
    later_pos = lax.broadcasted_iota(jnp.int32, (LEN, LEN), 1)
    earlier = lax.broadcasted_iota(jnp.int32, (LEN, LEN), 0)
    weights = jnp.where(later_pos >= earlier, jnp.exp((later_pos - earlier).astype(jnp.float32) * math.log(gae_decay)), jnp.float32(0.0))
    advantages = jnp.dot(weights, td_error, precision=lax.Precision.HIGHEST)
    prob_ratio = jnp.exp(scores[3] - scores[0])
    token_grad = -(loss_scale / SEQS) * live_float * (prob_ratio * advantages - penalty_gain * (prob_ratio - 1.0))
    soft_probs = jnp.exp(logits - log_norm[:, None])
    vocab_cols = lax.broadcasted_iota(jnp.int32, (LEN * SEQS, VOCAB), 1)
    target_hit = (vocab_cols == flat_ids[:, None]).astype(jnp.float32)
    slope = (token_grad.reshape(LEN * SEQS)[:, None] * (target_hit - soft_probs)).astype(jnp.bfloat16)
    grad_rows = lax.dot_general(slope, head_slices[3], (((1,), (1,)), ((), ())), preferred_element_type=jnp.float32)
    trunk_grad = jnp.zeros((N_SECTION, LEN, SEQS, D), jnp.bfloat16)
    trunk_grad = trunk_grad.at[3].set(grad_rows.reshape(LEN, SEQS, D).astype(jnp.bfloat16))
    return scores, advantages, trunk_grad
```

```python
import functools
import math

import jax
import jax.numpy as jnp
from jax import lax
from jax.experimental import pallas as pl
from jax.experimental.pallas import tpu as pltpu
from jax.sharding import PartitionSpec as P

gae_decay = 0.95
reward_gain = 0.5
drift_gain = 0.1
penalty_gain = 0.2
loss_scale = 16.0

MESH = pl.DeviceIdType.MESH
f32 = jnp.float32
bf16 = jnp.bfloat16


def each(count, fn):
    if count <= 9:
        for o in range(1, count):
            fn(o)
    else:
        lax.fori_loop(1, count, lambda o, carry: (fn(o), carry)[1], 0)


def kernel(
    cfg,
    hid_ref,
    tok_ref,
    len_ref,
    head_ref,
    vh_ref,
    score_out,
    adv_out,
    trunk_out,
    head_v,
    buf,
    tokbuf,
    statbuf,
    zbuf,
    ab,
    pf,
    s1,
    r1,
    s2,
    r2,
    hid_sem,
    head_sem,
    zrow_s,
    zrow_r,
    row_s,
    row_r,
    tok_s,
    tok_r,
    stat_s,
    stat_r,
    zs_s,
    zs_r,
    r1_s,
    r1_r,
    r2_s,
    r2_r,
):
    S, DP, MP, per, D, V, SEQ, C, C2, TILE = cfg
    PL = DP * MP
    G = PL // 2
    R = PL * per
    Rp = statbuf.shape[2]
    LEN = per * MP
    Kc = D // C
    Dc = D // C2
    sec = lax.axis_index("section")
    dp = lax.axis_index("dp")
    mp = lax.axis_index("mp")
    core = lax.rem(dp, 2)
    q = dp * MP + mp
    g = (dp // 2) * MP + mp
    partner = {"dp": dp + 1 - 2 * core, "mp": mp}
    partner_q = (dp + 1 - 2 * core) * MP + mp

    def plane_dev(o):
        i = lax.rem(q + o, PL)
        return {"dp": i // MP, "mp": lax.rem(i, MP)}, i

    def chip_dev(o, which):
        i = lax.rem(g + o, G)
        d = (i // MP) * 2 + which
        m = lax.rem(i, MP)
        return {"dp": d, "mp": m}, d * MP + m, i

    def sec_dev(o):
        i = lax.rem(sec + o, S)
        return {"section": i}, i

    def rc(src, dst, ss, rs, dev):
        return pltpu.make_async_remote_copy(
            src_ref=src, dst_ref=dst, send_sem=ss, recv_sem=rs, device_id=dev, device_id_type=MESH
        )

    def head_copy(c):
        cut = pl.ds(c * Kc, Kc)
        return pltpu.make_async_copy(head_ref.at[0, cut, :], head_v.at[cut, :], head_sem.at[c])

    hid_copy = pltpu.make_async_copy(hid_ref, buf.at[q], hid_sem)

    @pl.when(sec == 0)
    def _():
        hid_copy.start()

    for c in range(C):
        head_copy(c).start()

    tokbuf[q] = jnp.broadcast_to(tok_ref[...], (per, 128))

    barrier = pltpu.get_barrier_semaphore()

    def greet_plane(o):
        pl.semaphore_signal(barrier, inc=1, device_id=plane_dev(o)[0], device_id_type=MESH)

    def greet_section(o):
        pl.semaphore_signal(barrier, inc=1, device_id=sec_dev(o)[0], device_id_type=MESH)

    each(S, greet_section)
    each(PL, greet_plane)
    pl.semaphore_wait(barrier, PL - 1 + S - 1)

    def piece(slot, c):
        return buf.at[slot, :, pl.ds(c * Kc, Kc)]

    def z_copy(c, s):
        return rc(piece(q, c), piece(q, c), zrow_s.at[c, s], zrow_r.at[c], {"section": s})

    def own_to_partner(c):
        return rc(piece(q, c), piece(q, c), row_s.at[c, 0], row_r.at[c, q], partner)

    def own_to_chip(c, o):
        return rc(piece(q, c), piece(q, c), row_s.at[c, o], row_r.at[c, q], chip_dev(o, core)[0])

    def forward(c, o):
        i = chip_dev(o, core)[1]
        return rc(piece(i, c), piece(i, c), row_s.at[c, G - 1 + o], row_r.at[c, i], partner)

    def arrived(c, i):
        rc(piece(i, c), piece(i, c), row_s.at[c, 0], row_r.at[c, i], partner).wait_recv()

    def tok_copy(o):
        return rc(tokbuf.at[q], tokbuf.at[q], tok_s.at[o], tok_r.at[q], plane_dev(o)[0])

    def spread(c):
        @pl.when(sec == 0)
        def _():
            for s in range(S - 1, 0, -1):
                z_copy(c, s).start()

        @pl.when(sec != 0)
        def _():
            z_copy(c, 0).wait_recv()

        each(G, lambda o: own_to_chip(c, o).start())
        own_to_partner(c).start()

    def relay(c):
        def one(o):
            arrived(c, chip_dev(o, core)[1])
            forward(c, o).start()

        each(G, one)

    def settle(c):
        arrived(c, partner_q)
        each(G, lambda o: arrived(c, chip_dev(o, 1 - core)[1]))

    @pl.when(sec == 0)
    def _():
        hid_copy.wait()

    logits = jnp.zeros((R, V), f32)
    values = jnp.zeros((R, 1), f32)
    for step in range(C + 2):
        if step < C:
            spread(step)
        if step == 0:
            each(PL, lambda o: tok_copy(o).start())
        if 0 <= step - 1 < C:
            relay(step - 1)
        c = step - 2
        if c >= 0:
            settle(c)
            head_copy(c).wait()
            x = buf[:, :, c * Kc : (c + 1) * Kc].astype(f32).reshape(R, Kc)
            logits = logits + jnp.dot(
                x.astype(bf16), head_v[c * Kc : (c + 1) * Kc, :], preferred_element_type=f32
            )
            values = values + jnp.sum(
                x * vh_ref[:, c * Kc : (c + 1) * Kc].astype(f32), axis=1, keepdims=True
            )

    def tok_arrived(o):
        i = plane_dev(o)[1]
        rc(tokbuf.at[i], tokbuf.at[i], tok_s.at[o], tok_r.at[i], plane_dev(o)[0]).wait_recv()

    each(PL, tok_arrived)

    ids = tokbuf[...].reshape(R, 128)[:, :1] - q * V
    hit = lax.broadcasted_iota(jnp.int32, (R, V), 1) == ids
    m_col = jnp.max(logits, axis=1, keepdims=True)
    e = jnp.exp(logits - m_col)
    l_col = jnp.sum(e, axis=1, keepdims=True)
    p_col = jnp.sum(jnp.where(hit, logits, 0.0), axis=1, keepdims=True)
    eye = lax.broadcasted_iota(jnp.int32, (R, Rp), 0) == lax.broadcasted_iota(
        jnp.int32, (R, Rp), 1
    )

    def to_lanes(col):
        return jnp.sum(jnp.where(eye, col, 0.0), axis=0, keepdims=True)

    def to_column(row):
        return jnp.sum(jnp.where(eye, row, 0.0), axis=1, keepdims=True)

    sub = lax.broadcasted_iota(jnp.int32, (8, Rp), 0)
    m_lane = to_lanes(m_col)
    statbuf[q] = jnp.where(
        sub == 0, m_lane, jnp.where(sub == 1, to_lanes(l_col), to_lanes(p_col))
    )

    def stat_copy(o):
        return rc(statbuf.at[q], statbuf.at[q], stat_s.at[o], stat_r.at[q], plane_dev(o)[0])

    each(PL, lambda o: stat_copy(o).start())

    @pl.when(sec == S - 1)
    def _():
        both = jnp.concatenate(
            [jnp.where(hit, 0.0, e).astype(bf16), hit.astype(f32).astype(bf16)], axis=0
        )

        def tile(t, carry):
            cut = pl.ds(pl.multiple_of(t * TILE, TILE), TILE)
            ab[:, cut] = lax.dot_general(
                both, head_v[cut, :], (((1,), (1,)), ((), ())), preferred_element_type=f32
            )
            return carry

        lax.fori_loop(0, D // TILE, tile, 0)

    def stat_arrived(o):
        dev, i = plane_dev(o)
        rc(statbuf.at[i], statbuf.at[i], stat_s.at[o], stat_r.at[i], dev).wait_recv()

    each(PL, stat_arrived)
    st = statbuf[...]
    m_all = st[:, 0:1, :]
    m_top = jnp.max(m_all, axis=0)
    l_top = jnp.sum(st[:, 1:2, :] * jnp.exp(m_all - m_top[None]), axis=0)
    picked = jnp.sum(st[:, 2:3, :], axis=0)
    log_norm = m_top + jnp.log(l_top)
    raw = picked - log_norm

    lane = lax.broadcasted_iota(jnp.int32, (1, Rp), 1)
    seq_of = lane // LEN
    length_of = jnp.zeros((1, Rp), jnp.int32)
    for j in range(SEQ):
        length_of = length_of + jnp.where(seq_of == j, len_ref[j], 0)
    live = (lane - seq_of * LEN) < length_of
    scored = jnp.where(live, raw, 0.0)
    zbuf[sec] = jnp.where(sub == 0, scored, to_lanes(values))

    def zs_copy(o):
        return rc(zbuf.at[sec], zbuf.at[sec], zs_s.at[o], zs_r.at[sec], sec_dev(o)[0])

    each(S, lambda o: zs_copy(o).start())

    def s2_copy(c, o):
        dev, _, i = chip_dev(o, core)
        return rc(s2.at[c, i], r2.at[c, g], r2_s.at[c, o], r2_r.at[c, g], dev)

    @pl.when(sec == S - 1)
    def _():
        s_col = to_column(jnp.exp(m_lane - log_norm))
        t_col = to_column(1.0 - jnp.exp(raw))
        for c in range(C2):
            cut = slice(c * Dc, (c + 1) * Dc)
            pf[c] = (t_col * ab[R:, cut] - s_col * ab[:R, cut]).reshape(
                DP // 2, 2, MP, per, Dc
            )
            for i in range(DP // 2):
                s1[c, i * MP : (i + 1) * MP] = pf[c, i, 1 - core].astype(bf16)
            rc(s1.at[c], r1.at[c], r1_s.at[c], r1_r.at[c], partner).start()
        for c in range(C2):
            rc(s1.at[c], r1.at[c], r1_s.at[c], r1_r.at[c], partner).wait_recv()
            for i in range(DP // 2):
                s2[c, i * MP : (i + 1) * MP] = (
                    pf[c, i, core] + r1[c, i * MP : (i + 1) * MP].astype(f32)
                ).astype(bf16)
            each(G, lambda o: s2_copy(c, o).start())

    def zs_arrived(o):
        dev, i = sec_dev(o)
        rc(zbuf.at[i], zbuf.at[i], zs_s.at[o], zs_r.at[i], dev).wait_recv()

    each(S, zs_arrived)
    behaviour = zbuf[0][0:1]
    implicit = zbuf[1][0:1]
    anchor = zbuf[2][0:1]
    current = zbuf[S - 1][0:1]
    critic = jnp.where(live, zbuf[1][1:2], 0.0)
    reward = reward_gain * (implicit - anchor) - drift_gain * (behaviour - anchor)
    base = jnp.where(live, reward - critic, 0.0)
    later = lax.broadcasted_iota(jnp.int32, (Rp, Rp), 0)
    earlier = lax.broadcasted_iota(jnp.int32, (Rp, Rp), 1)
    gap = later - earlier
    same = (later // LEN) == (earlier // LEN)
    decay = math.log(gae_decay)
    weights = jnp.where(same & (gap >= 0), jnp.exp(gap.astype(f32) * decay), 0.0)
    shifted = jnp.where(same & (gap >= 1), jnp.exp((gap - 1).astype(f32) * decay), 0.0)
    advantage = (
        jnp.dot(
            jnp.broadcast_to(base, (8, Rp)),
            weights,
            precision=lax.Precision.HIGHEST,
            preferred_element_type=f32,
        )
        + jnp.dot(
            jnp.broadcast_to(critic, (8, Rp)),
            shifted,
            precision=lax.Precision.HIGHEST,
            preferred_element_type=f32,
        )
    )[0:1]
    prob_ratio = jnp.exp(current - behaviour)
    coeff = jnp.where(
        live,
        -(loss_scale / SEQ) * (prob_ratio * advantage - penalty_gain * (prob_ratio - 1.0)),
        0.0,
    )
    own = lax.broadcasted_iota(jnp.int32, (per, Rp), 1) == (
        lax.broadcasted_iota(jnp.int32, (per, Rp), 0) + q * per
    )

    def own_column(row):
        return jnp.sum(jnp.where(own, row, 0.0), axis=1, keepdims=True)

    score_out[0] = own_column(scored)
    adv_out[...] = own_column(advantage)

    @pl.when(sec != S - 1)
    def _():
        trunk_out[...] = jnp.zeros_like(trunk_out)

    @pl.when(sec == S - 1)
    def _():
        factor = own_column(coeff)
        for c in range(C2):

            def r2_arrived(o):
                dev, _, i = chip_dev(o, core)
                rc(s2.at[c, i], r2.at[c, i], r2_s.at[c, o], r2_r.at[c, i], dev).wait_recv()

            each(G, r2_arrived)
            total = pf[c, dp // 2, core, mp] + r1[c, g].astype(f32)
            if G <= 9:
                for o in range(1, G):
                    total = total + r2[c, chip_dev(o, core)[2]].astype(f32)
            else:
                total = lax.fori_loop(
                    1, G, lambda o, t: t + r2[c, chip_dev(o, core)[2]].astype(f32), total
                )
            trunk_out[:, c * Dc : (c + 1) * Dc] = (total * factor).astype(bf16)
        for c in range(C2):
            rc(s1.at[c], r1.at[c], r1_s.at[c], r1_r.at[c], partner).wait_send()
            each(G, lambda o: s2_copy(c, o).wait_send())

    for c in range(C):

        @pl.when(sec == 0)
        def _():
            for s in range(1, S):
                z_copy(c, s).wait_send()

        own_to_partner(c).wait_send()
        each(G, lambda o: own_to_chip(c, o).wait_send())
        each(G, lambda o: forward(c, o).wait_send())
    each(PL, lambda o: tok_copy(o).wait_send())
    each(PL, lambda o: stat_copy(o).wait_send())
    each(S, lambda o: zs_copy(o).wait_send())


def local(hidden, token_ids, seq_lengths, head_slices, value_head):
    S = lax.axis_size("section")
    DP = lax.axis_size("dp")
    MP = lax.axis_size("mp")
    PL = DP * MP
    G = PL // 2
    per, D = hidden.shape[1], hidden.shape[3]
    V = head_slices.shape[2]
    SEQ = seq_lengths.shape[0]
    C, C2 = 4, 2
    TILE = min(512, D)
    R = PL * per
    Rp = -(-R // 128) * 128
    dma = pltpu.SemaphoreType.DMA
    vmem = pl.BlockSpec(memory_space=pltpu.VMEM)
    anym = pl.BlockSpec(memory_space=pl.ANY)
    scores, adv, trunk = pl.pallas_call(
        functools.partial(kernel, (S, DP, MP, per, D, V, SEQ, C, C2, TILE)),
        out_shape=(
            jax.ShapeDtypeStruct((1, per, 1), f32),
            jax.ShapeDtypeStruct((per, 1), f32),
            jax.ShapeDtypeStruct((per, D), bf16),
        ),
        in_specs=[anym, vmem, pl.BlockSpec(memory_space=pltpu.SMEM), anym, vmem],
        out_specs=(vmem, vmem, vmem),
        scratch_shapes=[
            pltpu.VMEM((D, V), bf16),
            pltpu.VMEM((PL, per, D), bf16),
            pltpu.VMEM((PL, per, 128), jnp.int32),
            pltpu.VMEM((PL, 8, Rp), f32),
            pltpu.VMEM((S, 8, Rp), f32),
            pltpu.VMEM((2 * R, D), f32),
            pltpu.VMEM((C2, DP // 2, 2, MP, per, D // C2), f32),
            pltpu.VMEM((C2, G, per, D // C2), bf16),
            pltpu.VMEM((C2, G, per, D // C2), bf16),
            pltpu.VMEM((C2, G, per, D // C2), bf16),
            pltpu.VMEM((C2, G, per, D // C2), bf16),
            dma(()),
            dma((C,)),
            dma((C, S)),
            dma((C,)),
            dma((C, 2 * G)),
            dma((C, PL)),
            dma((PL,)),
            dma((PL,)),
            dma((PL,)),
            dma((PL,)),
            dma((S,)),
            dma((S,)),
            dma((C2,)),
            dma((C2,)),
            dma((C2, G)),
            dma((C2, G)),
        ],
        compiler_params=pltpu.CompilerParams(
            collective_id=0, has_side_effects=True, vmem_limit_bytes=60 * 1024 * 1024
        ),
    )(hidden.reshape(per, D), token_ids, seq_lengths, head_slices, value_head)
    return scores, adv, trunk.reshape(1, per, 1, D)


def solution(mesh):
    return jax.shard_map(
        local,
        mesh=mesh,
        in_specs=(
            P("section", "mp", "dp", None),
            P("mp", "dp"),
            P(),
            P("section", None, ("dp", "mp")),
            P("section", None),
        ),
        out_specs=(P("section", "mp", "dp"), P("mp", "dp"), P("section", "mp", "dp", None)),
        check_vma=False,
    )
```

```python
import functools
import math

import jax
import jax.numpy as jnp
from jax import lax
from jax.experimental import pallas as pl
from jax.experimental.pallas import tpu as pltpu
from jax.sharding import PartitionSpec as P

gae_decay = 0.95
reward_gain = 0.5
drift_gain = 0.1
penalty_gain = 0.2
loss_scale = 16.0

MESH = pl.DeviceIdType.MESH
f32 = jnp.float32
bf16 = jnp.bfloat16


def each(count, fn):
    if count <= 9:
        for o in range(1, count):
            fn(o)
    else:
        lax.fori_loop(1, count, lambda o, carry: (fn(o), carry)[1], 0)


def kernel(
    cfg,
    hid_ref,
    tok_ref,
    len_ref,
    head_ref,
    vh_ref,
    score_out,
    adv_out,
    trunk_out,
    head_v,
    buf,
    tokbuf,
    statbuf,
    zbuf,
    ab,
    pf,
    s1,
    r1,
    s2,
    r2,
    hid_sem,
    head_sem,
    zrow_s,
    zrow_r,
    row_s,
    row_r,
    tok_s,
    tok_r,
    stat_s,
    stat_r,
    zs_s,
    zs_r,
    r1_s,
    r1_r,
    r2_s,
    r2_r,
):
    S, DP, MP, per, D, V, SEQ, C, C2, TILE = cfg
    PL = DP * MP
    G = PL // 2
    R = PL * per
    Rp = statbuf.shape[2]
    LEN = per * MP
    Kc = D // C
    Dc = D // C2
    sec = lax.axis_index("section")
    dp = lax.axis_index("dp")
    mp = lax.axis_index("mp")
    core = lax.rem(dp, 2)
    q = dp * MP + mp
    g = (dp // 2) * MP + mp
    partner = {"dp": dp + 1 - 2 * core, "mp": mp}
    partner_q = (dp + 1 - 2 * core) * MP + mp

    def plane_dev(o):
        i = lax.rem(q + o, PL)
        return {"dp": i // MP, "mp": lax.rem(i, MP)}, i

    def chip_dev(o, which):
        i = lax.rem(g + o, G)
        d = (i // MP) * 2 + which
        m = lax.rem(i, MP)
        return {"dp": d, "mp": m}, d * MP + m, i

    def sec_dev(o):
        i = lax.rem(sec + o, S)
        return {"section": i}, i

    def rc(src, dst, ss, rs, dev):
        return pltpu.make_async_remote_copy(
            src_ref=src, dst_ref=dst, send_sem=ss, recv_sem=rs, device_id=dev, device_id_type=MESH
        )

    def head_copy(c):
        cut = pl.ds(c * Kc, Kc)
        return pltpu.make_async_copy(head_ref.at[0, cut, :], head_v.at[cut, :], head_sem.at[c])

    hid_copy = pltpu.make_async_copy(hid_ref, buf.at[q], hid_sem)

    @pl.when(sec == 0)
    def _():
        hid_copy.start()

    for c in range(C):
        head_copy(c).start()

    corner = lax.broadcasted_iota(jnp.int32, (per, per), 0) == lax.broadcasted_iota(
        jnp.int32, (per, per), 1
    )
    tok_col = jnp.sum(jnp.where(corner, tok_ref[...].astype(f32), 0.0), axis=1, keepdims=True)
    tokbuf[q] = jnp.broadcast_to(tok_col.astype(jnp.int32), (per, 128))

    barrier = pltpu.get_barrier_semaphore()

    def greet_plane(o):
        pl.semaphore_signal(barrier, inc=1, device_id=plane_dev(o)[0], device_id_type=MESH)

    def greet_section(o):
        pl.semaphore_signal(barrier, inc=1, device_id=sec_dev(o)[0], device_id_type=MESH)

    each(S, greet_section)
    each(PL, greet_plane)
    pl.semaphore_wait(barrier, PL - 1 + S - 1)

    def piece(slot, c):
        return buf.at[slot, :, pl.ds(c * Kc, Kc)]

    def z_copy(c, s):
        return rc(piece(q, c), piece(q, c), zrow_s.at[c, s], zrow_r.at[c], {"section": s})

    def own_to_partner(c):
        return rc(piece(q, c), piece(q, c), row_s.at[c, 0], row_r.at[c, q], partner)

    def own_to_chip(c, o):
        return rc(piece(q, c), piece(q, c), row_s.at[c, o], row_r.at[c, q], chip_dev(o, core)[0])

    def forward(c, o):
        i = chip_dev(o, core)[1]
        return rc(piece(i, c), piece(i, c), row_s.at[c, G - 1 + o], row_r.at[c, i], partner)

    def arrived(c, i):
        rc(piece(i, c), piece(i, c), row_s.at[c, 0], row_r.at[c, i], partner).wait_recv()

    def tok_copy(o):
        return rc(tokbuf.at[q], tokbuf.at[q], tok_s.at[o], tok_r.at[q], plane_dev(o)[0])

    def spread(c):
        @pl.when(sec == 0)
        def _():
            for s in range(S - 1, 0, -1):
                z_copy(c, s).start()

        @pl.when(sec != 0)
        def _():
            z_copy(c, 0).wait_recv()

        each(G, lambda o: own_to_chip(c, o).start())
        own_to_partner(c).start()

    def relay(c):
        def one(o):
            arrived(c, chip_dev(o, core)[1])
            forward(c, o).start()

        each(G, one)

    def settle(c):
        arrived(c, partner_q)
        each(G, lambda o: arrived(c, chip_dev(o, 1 - core)[1]))

    @pl.when(sec == 0)
    def _():
        hid_copy.wait()

    logits = jnp.zeros((R, V), f32)
    values = jnp.zeros((R, 1), f32)
    for step in range(C + 2):
        if step < C:
            spread(step)
        if step == 0:
            each(PL, lambda o: tok_copy(o).start())
        if 0 <= step - 1 < C:
            relay(step - 1)
        c = step - 2
        if c >= 0:
            settle(c)
            head_copy(c).wait()
            x = buf[:, :, c * Kc : (c + 1) * Kc].astype(f32).reshape(R, Kc)
            logits = logits + jnp.dot(
                x.astype(bf16), head_v[c * Kc : (c + 1) * Kc, :], preferred_element_type=f32
            )
            values = values + jnp.sum(
                x * vh_ref[:, c * Kc : (c + 1) * Kc].astype(f32), axis=1, keepdims=True
            )

    def tok_arrived(o):
        i = plane_dev(o)[1]
        rc(tokbuf.at[i], tokbuf.at[i], tok_s.at[o], tok_r.at[i], plane_dev(o)[0]).wait_recv()

    each(PL, tok_arrived)

    ids = tokbuf[...].reshape(R, 128)[:, :1] - q * V
    hit = lax.broadcasted_iota(jnp.int32, (R, V), 1) == ids
    m_col = jnp.max(logits, axis=1, keepdims=True)
    e = jnp.exp(logits - m_col)
    l_col = jnp.sum(e, axis=1, keepdims=True)
    p_col = jnp.sum(jnp.where(hit, logits, 0.0), axis=1, keepdims=True)
    eye = lax.broadcasted_iota(jnp.int32, (R, Rp), 0) == lax.broadcasted_iota(
        jnp.int32, (R, Rp), 1
    )

    def to_lanes(col):
        return jnp.sum(jnp.where(eye, col, 0.0), axis=0, keepdims=True)

    def to_column(row):
        return jnp.sum(jnp.where(eye, row, 0.0), axis=1, keepdims=True)

    sub = lax.broadcasted_iota(jnp.int32, (8, Rp), 0)
    m_lane = to_lanes(m_col)
    statbuf[q] = jnp.where(
        sub == 0, m_lane, jnp.where(sub == 1, to_lanes(l_col), to_lanes(p_col))
    )

    def stat_copy(o):
        return rc(statbuf.at[q], statbuf.at[q], stat_s.at[o], stat_r.at[q], plane_dev(o)[0])

    each(PL, lambda o: stat_copy(o).start())

    @pl.when(sec == S - 1)
    def _():
        both = jnp.concatenate(
            [jnp.where(hit, 0.0, e).astype(bf16), hit.astype(f32).astype(bf16)], axis=0
        )

        def tile(t, carry):
            cut = pl.ds(pl.multiple_of(t * TILE, TILE), TILE)
            ab[:, cut] = lax.dot_general(
                both, head_v[cut, :], (((1,), (1,)), ((), ())), preferred_element_type=f32
            )
            return carry

        lax.fori_loop(0, D // TILE, tile, 0)

    def stat_arrived(o):
        dev, i = plane_dev(o)
        rc(statbuf.at[i], statbuf.at[i], stat_s.at[o], stat_r.at[i], dev).wait_recv()

    each(PL, stat_arrived)
    st = statbuf[...]
    m_all = st[:, 0:1, :]
    m_top = jnp.max(m_all, axis=0)
    l_top = jnp.sum(st[:, 1:2, :] * jnp.exp(m_all - m_top[None]), axis=0)
    picked = jnp.sum(st[:, 2:3, :], axis=0)
    log_norm = m_top + jnp.log(l_top)
    raw = picked - log_norm

    lane = lax.broadcasted_iota(jnp.int32, (1, Rp), 1)
    seq_of = lane // LEN
    length_of = jnp.zeros((1, Rp), jnp.int32)
    for j in range(SEQ):
        length_of = length_of + jnp.where(seq_of == j, len_ref[j], 0)
    live = (lane - seq_of * LEN) < length_of
    scored = jnp.where(live, raw, 0.0)
    zbuf[sec] = jnp.where(sub == 0, scored, to_lanes(values))

    def zs_copy(o):
        return rc(zbuf.at[sec], zbuf.at[sec], zs_s.at[o], zs_r.at[sec], sec_dev(o)[0])

    each(S, lambda o: zs_copy(o).start())

    def s2_copy(c, o):
        dev, _, i = chip_dev(o, core)
        return rc(s2.at[c, i], r2.at[c, g], r2_s.at[c, o], r2_r.at[c, g], dev)

    @pl.when(sec == S - 1)
    def _():
        s_col = to_column(jnp.exp(m_lane - log_norm))
        t_col = to_column(1.0 - jnp.exp(raw))
        for c in range(C2):
            cut = slice(c * Dc, (c + 1) * Dc)
            pf[c] = (t_col * ab[R:, cut] - s_col * ab[:R, cut]).reshape(
                DP // 2, 2, MP, per, Dc
            )
            for i in range(DP // 2):
                s1[c, i * MP : (i + 1) * MP] = pf[c, i, 1 - core].astype(bf16)
            rc(s1.at[c], r1.at[c], r1_s.at[c], r1_r.at[c], partner).start()
        for c in range(C2):
            rc(s1.at[c], r1.at[c], r1_s.at[c], r1_r.at[c], partner).wait_recv()
            for i in range(DP // 2):
                s2[c, i * MP : (i + 1) * MP] = (
                    pf[c, i, core] + r1[c, i * MP : (i + 1) * MP].astype(f32)
                ).astype(bf16)
            each(G, lambda o: s2_copy(c, o).start())

    def zs_arrived(o):
        dev, i = sec_dev(o)
        rc(zbuf.at[i], zbuf.at[i], zs_s.at[o], zs_r.at[i], dev).wait_recv()

    each(S, zs_arrived)
    behaviour = zbuf[0][0:1]
    implicit = zbuf[1][0:1]
    anchor = zbuf[2][0:1]
    current = zbuf[S - 1][0:1]
    critic = jnp.where(live, zbuf[1][1:2], 0.0)
    reward = reward_gain * (implicit - anchor) - drift_gain * (behaviour - anchor)
    base = jnp.where(live, reward - critic, 0.0)
    later = lax.broadcasted_iota(jnp.int32, (Rp, Rp), 0)
    earlier = lax.broadcasted_iota(jnp.int32, (Rp, Rp), 1)
    gap = later - earlier
    same = (later // LEN) == (earlier // LEN)
    decay = math.log(gae_decay)
    weights = jnp.where(same & (gap >= 0), jnp.exp(gap.astype(f32) * decay), 0.0)
    shifted = jnp.where(same & (gap >= 1), jnp.exp((gap - 1).astype(f32) * decay), 0.0)
    advantage = (
        jnp.dot(
            jnp.broadcast_to(base, (8, Rp)),
            weights,
            precision=lax.Precision.HIGHEST,
            preferred_element_type=f32,
        )
        + jnp.dot(
            jnp.broadcast_to(critic, (8, Rp)),
            shifted,
            precision=lax.Precision.HIGHEST,
            preferred_element_type=f32,
        )
    )[0:1]
    prob_ratio = jnp.exp(current - behaviour)
    coeff = jnp.where(
        live,
        -(loss_scale / SEQ) * (prob_ratio * advantage - penalty_gain * (prob_ratio - 1.0)),
        0.0,
    )
    own = lax.broadcasted_iota(jnp.int32, (per, Rp), 1) == (
        lax.broadcasted_iota(jnp.int32, (per, Rp), 0) + q * per
    )

    def own_column(row):
        return jnp.sum(jnp.where(own, row, 0.0), axis=1, keepdims=True)

    def own_row(row):
        return jnp.sum(jnp.where(corner, own_column(row), 0.0), axis=0, keepdims=True)

    score_out[...] = own_row(scored)
    adv_out[...] = own_row(advantage)

    @pl.when(sec != S - 1)
    def _():
        trunk_out[...] = jnp.zeros_like(trunk_out)

    @pl.when(sec == S - 1)
    def _():
        factor = own_column(coeff)
        for c in range(C2):

            def r2_arrived(o):
                dev, _, i = chip_dev(o, core)
                rc(s2.at[c, i], r2.at[c, i], r2_s.at[c, o], r2_r.at[c, i], dev).wait_recv()

            each(G, r2_arrived)
            total = pf[c, dp // 2, core, mp] + r1[c, g].astype(f32)
            if G <= 9:
                for o in range(1, G):
                    total = total + r2[c, chip_dev(o, core)[2]].astype(f32)
            else:
                total = lax.fori_loop(
                    1, G, lambda o, t: t + r2[c, chip_dev(o, core)[2]].astype(f32), total
                )
            trunk_out[:, c * Dc : (c + 1) * Dc] = (total * factor).astype(bf16)
        for c in range(C2):
            rc(s1.at[c], r1.at[c], r1_s.at[c], r1_r.at[c], partner).wait_send()
            each(G, lambda o: s2_copy(c, o).wait_send())

    for c in range(C):

        @pl.when(sec == 0)
        def _():
            for s in range(1, S):
                z_copy(c, s).wait_send()

        own_to_partner(c).wait_send()
        each(G, lambda o: own_to_chip(c, o).wait_send())
        each(G, lambda o: forward(c, o).wait_send())
    each(PL, lambda o: tok_copy(o).wait_send())
    each(PL, lambda o: stat_copy(o).wait_send())
    each(S, lambda o: zs_copy(o).wait_send())


def local(hidden, token_ids, seq_lengths, head_slices, value_head):
    S = lax.axis_size("section")
    DP = lax.axis_size("dp")
    MP = lax.axis_size("mp")
    PL = DP * MP
    G = PL // 2
    per, D = hidden.shape[1], hidden.shape[3]
    V = head_slices.shape[2]
    SEQ = seq_lengths.shape[0]
    C, C2 = 1, 1
    TILE = min(512, D)
    R = PL * per
    Rp = -(-R // 128) * 128
    dma = pltpu.SemaphoreType.DMA
    vmem = pl.BlockSpec(memory_space=pltpu.VMEM)
    anym = pl.BlockSpec(memory_space=pl.ANY)
    scores, adv, trunk = pl.pallas_call(
        functools.partial(kernel, (S, DP, MP, per, D, V, SEQ, C, C2, TILE)),
        out_shape=(
            pltpu.VMEM((1, per), f32),
            pltpu.VMEM((1, per), f32),
            pltpu.VMEM((per, D), bf16),
        ),
        in_specs=[anym, vmem, pl.BlockSpec(memory_space=pltpu.SMEM), anym, vmem],
        out_specs=(vmem, vmem, vmem),
        scratch_shapes=[
            pltpu.VMEM((D, V), bf16),
            pltpu.VMEM((PL, per, D), bf16),
            pltpu.VMEM((PL, per, 128), jnp.int32),
            pltpu.VMEM((PL, 8, Rp), f32),
            pltpu.VMEM((S, 8, Rp), f32),
            pltpu.VMEM((2 * R, D), f32),
            pltpu.VMEM((C2, DP // 2, 2, MP, per, D // C2), f32),
            pltpu.VMEM((C2, G, per, D // C2), bf16),
            pltpu.VMEM((C2, G, per, D // C2), bf16),
            pltpu.VMEM((C2, G, per, D // C2), bf16),
            pltpu.VMEM((C2, G, per, D // C2), bf16),
            dma(()),
            dma((C,)),
            dma((C, S)),
            dma((C,)),
            dma((C, 2 * G)),
            dma((C, PL)),
            dma((PL,)),
            dma((PL,)),
            dma((PL,)),
            dma((PL,)),
            dma((S,)),
            dma((S,)),
            dma((C2,)),
            dma((C2,)),
            dma((C2, G)),
            dma((C2, G)),
        ],
        compiler_params=pltpu.CompilerParams(
            collective_id=0, has_side_effects=True, vmem_limit_bytes=60 * 1024 * 1024
        ),
    )(hidden.reshape(per, D), token_ids.reshape(1, per), seq_lengths, head_slices, value_head)
    return scores.reshape(1, per, 1), adv.reshape(per, 1), trunk.reshape(1, per, 1, D)


def solution(mesh):
    return jax.shard_map(
        local,
        mesh=mesh,
        in_specs=(
            P("section", "mp", "dp", None),
            P("mp", "dp"),
            P(),
            P("section", None, ("dp", "mp")),
            P("section", None),
        ),
        out_specs=(P("section", "mp", "dp"), P("mp", "dp"), P("section", "mp", "dp", None)),
        check_vma=False,
    )
```

```python
import functools
import math

import jax
import jax.numpy as jnp
from jax import lax
from jax.experimental import pallas as pl
from jax.experimental.pallas import tpu as pltpu
from jax.sharding import PartitionSpec as P

gae_decay = 0.95
reward_gain = 0.5
drift_gain = 0.1
penalty_gain = 0.2
loss_scale = 16.0

MESH = pl.DeviceIdType.MESH
f32 = jnp.float32
bf16 = jnp.bfloat16


def each(count, fn):
    if count <= 9:
        for o in range(1, count):
            fn(o)
    else:
        lax.fori_loop(1, count, lambda o, carry: (fn(o), carry)[1], 0)


def kernel(
    cfg,
    hid_ref,
    tok_ref,
    len_ref,
    head_ref,
    vh_ref,
    score_out,
    adv_out,
    trunk_out,
    head_v,
    buf,
    tokbuf,
    statbuf,
    zbuf,
    ab,
    pf,
    s1,
    r1,
    s2,
    r2,
    hid_sem,
    head_sem,
    zrow_s,
    zrow_r,
    row_s,
    row_r,
    tok_s,
    tok_r,
    stat_s,
    stat_r,
    zs_s,
    zs_r,
    r1_s,
    r1_r,
    r2_s,
    r2_r,
):
    S, DP, MP, per, D, V, SEQ, C, C2, TILE = cfg
    PL = DP * MP
    G = PL // 2
    R = PL * per
    Rp = statbuf.shape[2]
    LEN = per * MP
    Kc = D // C
    Dc = D // C2
    sec = lax.axis_index("section")
    dp = lax.axis_index("dp")
    mp = lax.axis_index("mp")
    core = lax.rem(dp, 2)
    q = dp * MP + mp
    g = (dp // 2) * MP + mp
    partner = {"dp": dp + 1 - 2 * core, "mp": mp}
    partner_q = (dp + 1 - 2 * core) * MP + mp

    def plane_dev(o):
        i = lax.rem(q + o, PL)
        return {"dp": i // MP, "mp": lax.rem(i, MP)}, i

    def chip_dev(o, which):
        i = lax.rem(g + o, G)
        d = (i // MP) * 2 + which
        m = lax.rem(i, MP)
        return {"dp": d, "mp": m}, d * MP + m, i

    def sec_dev(o):
        i = lax.rem(sec + o, S)
        return {"section": i}, i

    def rc(src, dst, ss, rs, dev):
        return pltpu.make_async_remote_copy(
            src_ref=src, dst_ref=dst, send_sem=ss, recv_sem=rs, device_id=dev, device_id_type=MESH
        )

    def head_copy(c):
        cut = pl.ds(c * Kc, Kc)
        return pltpu.make_async_copy(head_ref.at[0, cut, :], head_v.at[cut, :], head_sem.at[c])

    hid_copy = pltpu.make_async_copy(hid_ref, buf.at[q], hid_sem)

    @pl.when(sec == 0)
    def _():
        hid_copy.start()

    for c in range(C):
        head_copy(c).start()

    corner = lax.broadcasted_iota(jnp.int32, (per, per), 0) == lax.broadcasted_iota(
        jnp.int32, (per, per), 1
    )
    tok_col = jnp.sum(jnp.where(corner, tok_ref[...].astype(f32), 0.0), axis=1, keepdims=True)
    tokbuf[q] = jnp.broadcast_to(tok_col.astype(jnp.int32), (per, 128))

    barrier = pltpu.get_barrier_semaphore()

    def greet_plane(o):
        pl.semaphore_signal(barrier, inc=1, device_id=plane_dev(o)[0], device_id_type=MESH)

    def greet_section(o):
        pl.semaphore_signal(barrier, inc=1, device_id=sec_dev(o)[0], device_id_type=MESH)

    each(S, greet_section)
    each(PL, greet_plane)
    pl.semaphore_wait(barrier, PL - 1 + S - 1)

    def piece(slot, c):
        return buf.at[slot, :, pl.ds(c * Kc, Kc)]

    def z_copy(c, s):
        return rc(piece(q, c), piece(q, c), zrow_s.at[c, s], zrow_r.at[c], {"section": s})

    def own_to_partner(c):
        return rc(piece(q, c), piece(q, c), row_s.at[c, 0], row_r.at[c, q], partner)

    def own_to_chip(c, o):
        return rc(piece(q, c), piece(q, c), row_s.at[c, o], row_r.at[c, q], chip_dev(o, core)[0])

    def forward(c, o):
        i = chip_dev(o, core)[1]
        return rc(piece(i, c), piece(i, c), row_s.at[c, G - 1 + o], row_r.at[c, i], partner)

    def arrived(c, i):
        rc(piece(i, c), piece(i, c), row_s.at[c, 0], row_r.at[c, i], partner).wait_recv()

    def tok_copy(o):
        return rc(tokbuf.at[q], tokbuf.at[q], tok_s.at[o], tok_r.at[q], plane_dev(o)[0])

    def spread(c):
        @pl.when(sec == 0)
        def _():
            for s in range(S - 1, 0, -1):
                z_copy(c, s).start()

        if c == 0:
            each(PL, lambda o: tok_copy(o).start())

        @pl.when(sec != 0)
        def _():
            z_copy(c, 0).wait_recv()

        each(G, lambda o: own_to_chip(c, o).start())
        own_to_partner(c).start()

    def relay(c):
        def one(o):
            arrived(c, chip_dev(o, core)[1])
            forward(c, o).start()

        each(G, one)

    def settle(c):
        arrived(c, partner_q)
        each(G, lambda o: arrived(c, chip_dev(o, 1 - core)[1]))

    @pl.when(sec == 0)
    def _():
        hid_copy.wait()

    logits = jnp.zeros((R, V), f32)
    values = jnp.zeros((R, 1), f32)
    for step in range(C + 2):
        if step < C:
            spread(step)
        if 0 <= step - 1 < C:
            relay(step - 1)
        c = step - 2
        if c >= 0:
            settle(c)
            head_copy(c).wait()
            x = buf[:, :, c * Kc : (c + 1) * Kc].astype(f32).reshape(R, Kc)
            logits = logits + jnp.dot(
                x.astype(bf16), head_v[c * Kc : (c + 1) * Kc, :], preferred_element_type=f32
            )
            values = values + jnp.sum(
                x * vh_ref[:, c * Kc : (c + 1) * Kc].astype(f32), axis=1, keepdims=True
            )

    def tok_arrived(o):
        i = plane_dev(o)[1]
        rc(tokbuf.at[i], tokbuf.at[i], tok_s.at[o], tok_r.at[i], plane_dev(o)[0]).wait_recv()

    each(PL, tok_arrived)

    ids = tokbuf[...].reshape(R, 128)[:, :1] - q * V
    hit = lax.broadcasted_iota(jnp.int32, (R, V), 1) == ids
    m_col = jnp.max(logits, axis=1, keepdims=True)
    e = jnp.exp(logits - m_col)
    l_col = jnp.sum(e, axis=1, keepdims=True)
    p_col = jnp.sum(jnp.where(hit, logits, 0.0), axis=1, keepdims=True)
    eye = lax.broadcasted_iota(jnp.int32, (R, Rp), 0) == lax.broadcasted_iota(
        jnp.int32, (R, Rp), 1
    )

    def to_lanes(col):
        return jnp.sum(jnp.where(eye, col, 0.0), axis=0, keepdims=True)

    def to_column(row):
        return jnp.sum(jnp.where(eye, row, 0.0), axis=1, keepdims=True)

    sub = lax.broadcasted_iota(jnp.int32, (8, Rp), 0)
    m_lane = to_lanes(m_col)
    statbuf[q] = jnp.where(
        sub == 0, m_lane, jnp.where(sub == 1, to_lanes(l_col), to_lanes(p_col))
    )

    def stat_copy(o):
        return rc(statbuf.at[q], statbuf.at[q], stat_s.at[o], stat_r.at[q], plane_dev(o)[0])

    each(PL, lambda o: stat_copy(o).start())

    @pl.when(sec == S - 1)
    def _():
        both = jnp.concatenate(
            [jnp.where(hit, 0.0, e).astype(bf16), hit.astype(f32).astype(bf16)], axis=0
        )

        def tile(t, carry):
            cut = pl.ds(pl.multiple_of(t * TILE, TILE), TILE)
            ab[:, cut] = lax.dot_general(
                both, head_v[cut, :], (((1,), (1,)), ((), ())), preferred_element_type=f32
            )
            return carry

        lax.fori_loop(0, D // TILE, tile, 0)

    def stat_arrived(o):
        dev, i = plane_dev(o)
        rc(statbuf.at[i], statbuf.at[i], stat_s.at[o], stat_r.at[i], dev).wait_recv()

    each(PL, stat_arrived)
    st = statbuf[...]
    m_all = st[:, 0:1, :]
    m_top = jnp.max(m_all, axis=0)
    l_top = jnp.sum(st[:, 1:2, :] * jnp.exp(m_all - m_top[None]), axis=0)
    picked = jnp.sum(st[:, 2:3, :], axis=0)
    log_norm = m_top + jnp.log(l_top)
    raw = picked - log_norm

    lane = lax.broadcasted_iota(jnp.int32, (1, Rp), 1)
    seq_of = lane // LEN
    length_of = jnp.zeros((1, Rp), jnp.int32)
    for j in range(SEQ):
        length_of = length_of + jnp.where(seq_of == j, len_ref[j], 0)
    live = (lane - seq_of * LEN) < length_of
    scored = jnp.where(live, raw, 0.0)
    zbuf[sec] = jnp.where(sub == 0, scored, to_lanes(values))

    def zs_copy(o):
        return rc(zbuf.at[sec], zbuf.at[sec], zs_s.at[o], zs_r.at[sec], sec_dev(o)[0])

    each(S, lambda o: zs_copy(o).start())

    def s2_copy(c, o):
        dev, _, i = chip_dev(o, core)
        return rc(s2.at[c, i], r2.at[c, g], r2_s.at[c, o], r2_r.at[c, g], dev)

    @pl.when(sec == S - 1)
    def _():
        s_col = to_column(jnp.exp(m_lane - log_norm))
        t_col = to_column(1.0 - jnp.exp(raw))
        for c in range(C2):
            cut = slice(c * Dc, (c + 1) * Dc)
            pf[c] = (t_col * ab[R:, cut] - s_col * ab[:R, cut]).reshape(
                DP // 2, 2, MP, per, Dc
            )
            for i in range(DP // 2):
                s1[c, i * MP : (i + 1) * MP] = pf[c, i, 1 - core].astype(bf16)
            rc(s1.at[c], r1.at[c], r1_s.at[c], r1_r.at[c], partner).start()
        for c in range(C2):
            rc(s1.at[c], r1.at[c], r1_s.at[c], r1_r.at[c], partner).wait_recv()
            for i in range(DP // 2):
                s2[c, i * MP : (i + 1) * MP] = (
                    pf[c, i, core] + r1[c, i * MP : (i + 1) * MP].astype(f32)
                ).astype(bf16)
            each(G, lambda o: s2_copy(c, o).start())

    def zs_arrived(o):
        dev, i = sec_dev(o)
        rc(zbuf.at[i], zbuf.at[i], zs_s.at[o], zs_r.at[i], dev).wait_recv()

    each(S, zs_arrived)
    behaviour = zbuf[0][0:1]
    implicit = zbuf[1][0:1]
    anchor = zbuf[2][0:1]
    current = zbuf[S - 1][0:1]
    critic = jnp.where(live, zbuf[1][1:2], 0.0)
    reward = reward_gain * (implicit - anchor) - drift_gain * (behaviour - anchor)
    base = jnp.where(live, reward - critic, 0.0)
    later = lax.broadcasted_iota(jnp.int32, (Rp, Rp), 0)
    earlier = lax.broadcasted_iota(jnp.int32, (Rp, Rp), 1)
    gap = later - earlier
    same = (later // LEN) == (earlier // LEN)
    decay = math.log(gae_decay)
    weights = jnp.where(same & (gap >= 0), jnp.exp(gap.astype(f32) * decay), 0.0)
    shifted = jnp.where(same & (gap >= 1), jnp.exp((gap - 1).astype(f32) * decay), 0.0)
    advantage = (
        jnp.dot(
            jnp.broadcast_to(base, (8, Rp)),
            weights,
            precision=lax.Precision.HIGHEST,
            preferred_element_type=f32,
        )
        + jnp.dot(
            jnp.broadcast_to(critic, (8, Rp)),
            shifted,
            precision=lax.Precision.HIGHEST,
            preferred_element_type=f32,
        )
    )[0:1]
    prob_ratio = jnp.exp(current - behaviour)
    coeff = jnp.where(
        live,
        -(loss_scale / SEQ) * (prob_ratio * advantage - penalty_gain * (prob_ratio - 1.0)),
        0.0,
    )
    own = lax.broadcasted_iota(jnp.int32, (per, Rp), 1) == (
        lax.broadcasted_iota(jnp.int32, (per, Rp), 0) + q * per
    )

    def own_column(row):
        return jnp.sum(jnp.where(own, row, 0.0), axis=1, keepdims=True)

    def own_row(row):
        return jnp.sum(jnp.where(corner, own_column(row), 0.0), axis=0, keepdims=True)

    score_out[...] = own_row(scored)
    adv_out[...] = own_row(advantage)

    @pl.when(sec != S - 1)
    def _():
        trunk_out[...] = jnp.zeros_like(trunk_out)

    @pl.when(sec == S - 1)
    def _():
        factor = own_column(coeff)
        for c in range(C2):

            def r2_arrived(o):
                dev, _, i = chip_dev(o, core)
                rc(s2.at[c, i], r2.at[c, i], r2_s.at[c, o], r2_r.at[c, i], dev).wait_recv()

            each(G, r2_arrived)
            total = pf[c, dp // 2, core, mp] + r1[c, g].astype(f32)
            if G <= 9:
                for o in range(1, G):
                    total = total + r2[c, chip_dev(o, core)[2]].astype(f32)
            else:
                total = lax.fori_loop(
                    1, G, lambda o, t: t + r2[c, chip_dev(o, core)[2]].astype(f32), total
                )
            trunk_out[:, c * Dc : (c + 1) * Dc] = (total * factor).astype(bf16)
        for c in range(C2):
            rc(s1.at[c], r1.at[c], r1_s.at[c], r1_r.at[c], partner).wait_send()
            each(G, lambda o: s2_copy(c, o).wait_send())

    for c in range(C):

        @pl.when(sec == 0)
        def _():
            for s in range(1, S):
                z_copy(c, s).wait_send()

        own_to_partner(c).wait_send()
        each(G, lambda o: own_to_chip(c, o).wait_send())
        each(G, lambda o: forward(c, o).wait_send())
    each(PL, lambda o: tok_copy(o).wait_send())
    each(PL, lambda o: stat_copy(o).wait_send())
    each(S, lambda o: zs_copy(o).wait_send())


def hand_over(a_ref, b_ref, c_ref, a_out, b_out, c_out, sem):
    moves = [
        pltpu.make_async_copy(src, dst, sem.at[k])
        for k, (src, dst) in enumerate(((a_ref, a_out), (b_ref, b_out), (c_ref, c_out)))
    ]
    for move in moves:
        move.start()
    for move in moves:
        move.wait()


def local(hidden, token_ids, seq_lengths, head_slices, value_head):
    S = lax.axis_size("section")
    DP = lax.axis_size("dp")
    MP = lax.axis_size("mp")
    PL = DP * MP
    G = PL // 2
    per, D = hidden.shape[1], hidden.shape[3]
    V = head_slices.shape[2]
    SEQ = seq_lengths.shape[0]
    C, C2 = 1, 1
    TILE = min(512, D)
    R = PL * per
    Rp = -(-R // 128) * 128
    dma = pltpu.SemaphoreType.DMA
    vmem = pl.BlockSpec(memory_space=pltpu.VMEM)
    anym = pl.BlockSpec(memory_space=pl.ANY)
    scores, adv, trunk = pl.pallas_call(
        functools.partial(kernel, (S, DP, MP, per, D, V, SEQ, C, C2, TILE)),
        out_shape=(
            pltpu.VMEM((1, per), f32),
            pltpu.VMEM((1, per), f32),
            pltpu.VMEM((per, D), bf16),
        ),
        in_specs=[anym, vmem, pl.BlockSpec(memory_space=pltpu.SMEM), anym, vmem],
        out_specs=(vmem, vmem, vmem),
        scratch_shapes=[
            pltpu.VMEM((D, V), bf16),
            pltpu.VMEM((PL, per, D), bf16),
            pltpu.VMEM((PL, per, 128), jnp.int32),
            pltpu.VMEM((PL, 8, Rp), f32),
            pltpu.VMEM((S, 8, Rp), f32),
            pltpu.VMEM((2 * R, D), f32),
            pltpu.VMEM((C2, DP // 2, 2, MP, per, D // C2), f32),
            pltpu.VMEM((C2, G, per, D // C2), bf16),
            pltpu.VMEM((C2, G, per, D // C2), bf16),
            pltpu.VMEM((C2, G, per, D // C2), bf16),
            pltpu.VMEM((C2, G, per, D // C2), bf16),
            dma(()),
            dma((C,)),
            dma((C, S)),
            dma((C,)),
            dma((C, 2 * G)),
            dma((C, PL)),
            dma((PL,)),
            dma((PL,)),
            dma((PL,)),
            dma((PL,)),
            dma((S,)),
            dma((S,)),
            dma((C2,)),
            dma((C2,)),
            dma((C2, G)),
            dma((C2, G)),
        ],
        compiler_params=pltpu.CompilerParams(
            collective_id=0, has_side_effects=True, vmem_limit_bytes=60 * 1024 * 1024
        ),
    )(hidden.reshape(per, D), token_ids.reshape(1, per), seq_lengths, head_slices, value_head)
    scores, adv, trunk = pl.pallas_call(
        hand_over,
        out_shape=(
            jax.ShapeDtypeStruct((1, per), f32),
            jax.ShapeDtypeStruct((1, per), f32),
            jax.ShapeDtypeStruct((per, D), bf16),
        ),
        in_specs=[vmem] * 3,
        out_specs=[anym] * 3,
        scratch_shapes=[dma((3,))],
    )(*(pltpu.with_memory_space_constraint(v, pltpu.VMEM) for v in (scores, adv, trunk)))
    return scores.reshape(1, per, 1), adv.reshape(per, 1), trunk.reshape(1, per, 1, D)


def solution(mesh):
    return jax.shard_map(
        local,
        mesh=mesh,
        in_specs=(
            P("section", "mp", "dp", None),
            P("mp", "dp"),
            P(),
            P("section", None, ("dp", "mp")),
            P("section", None),
        ),
        out_specs=(P("section", "mp", "dp"), P("mp", "dp"), P("section", "mp", "dp", None)),
        check_vma=False,
    )
```
